256 devices in a mesh: ctx: 16 (over z, x_hi), head: 16 (over x_lo, y, core).
Axes of the slice: x: 4 (x_hi: 2, x_lo: 2; x = x_hi * 2 + x_lo), y: 4, z: 8, core: 2. Of those that a mesh axis runs over, the one named last changes fastest.
Arguments:
- hidden: bfloat16 [16384, 8192], P('ctx', 'head'), may hold values from -6 to 6
- query_frozen_projection: bfloat16 [16384, 8192], P('ctx', 'head'), may hold values from -20 to 20
- key_projected: bfloat16 [16384, 1024], P('ctx'), may hold values from -20 to 20
- value_frozen_projection: bfloat16 [16384, 1024], P('ctx'), may hold values from -6 to 6
- query_down_factor: bfloat16 [8192, 16], P('head'), may hold values from -0.0625 to 0.0625
- query_up_factor: bfloat16 [16, 8192], P(None, 'head'), may hold values from -1.5 to 1.5
- value_down_factor: bfloat16 [8192, 16], P('head'), may hold values from -0.0625 to 0.0625
- value_up_factor: bfloat16 [16, 1024], replicated, may hold values from -1.5 to 1.5
- output_gradient: bfloat16 [16384, 8192], P('ctx', 'head'), may hold values from -0.046875 to 0.046875
- head_shift_mask: int32 [64], P('head'), may hold values from 0 to 1, as said below
Outputs:
- grad_a_q: float32 [8192, 16], P('head')
- query_up_gradient: float32 [16, 8192], P(None, 'head')
- grad_a_v: float32 [8192, 16], P('head')
- value_up_gradient: float32 [16, 1024], replicated
The draws below stay inside these ranges and needn't reach their ends.
Inputs may be any that keep to these rules, and one draw needn't show every extreme that they name: `head_shift_mask`: exactly 32 of the heads carry 1.
All inputs are finite; a program needn't handle non-finite values.
Results may differ from the reference program's by a relative error of at most 0.0173.
The reference program's roundings to bfloat16 on the way count: a program that leaves them out, or rounds other values in their place, can miss the bound.
Values may be sent and summed in bfloat16 or wider, within the bound.
A program may use at most 128 MiB of HBM per device.

```python
import jax
import jax.numpy as jnp
from jax import lax

MODEL_WIDTH = 8192
QUERY_HEADS = 64
KEY_VALUE_HEADS = 8
HEAD_SIZE = 128
ADAPTER_RANK = 16
GROUP = 1024
SEQ = 16384


def base_keys(key):
    noise_rows = jnp.clip(jax.random.normal(jax.random.fold_in(key, 31), (SEQ, KEY_VALUE_HEADS * HEAD_SIZE), jnp.float32), -4.0, 4.0)
    return noise_rows


def draw_key_projected(key, part):
    noise_rows = base_keys(key)
    return noise_rows.astype(jnp.bfloat16)


def draw_query_frozen_projection(key, part):
    noise_rows = jnp.clip(jax.random.normal(jax.random.fold_in(key, 41), (SEQ, QUERY_HEADS * HEAD_SIZE), jnp.float32), -4.0, 4.0)
    return noise_rows.astype(jnp.bfloat16)


def draw_head_shift_mask(key, part):
    shuffled = jax.random.permutation(jax.random.fold_in(key, 51), QUERY_HEADS)
    return (shuffled < QUERY_HEADS // 2).astype(jnp.int32)


def shard_levels(rng, dims, shards, low, largest):
    loudness = 1.0
    for axis_at, shards_of in shards:
        heights = jax.random.uniform(jax.random.fold_in(jax.random.fold_in(rng, 6), axis_at), (shards_of,), jnp.float32, low / len(shards), largest / len(shards))
        loudness = loudness * jnp.repeat(jnp.exp(heights), dims[axis_at] // shards_of).reshape((-1,) + (1,) * (len(dims) - 1 - axis_at))
    return loudness


def bell_draw(own_key, extent, scale, most, cuts=(), kind=jnp.bfloat16):
    drawn = scale * jax.random.normal(own_key, extent, jnp.float32)
    if cuts:
        drawn = drawn * shard_levels(own_key, extent, cuts, -0.22, 0.18)
    return jnp.clip(drawn, -most, most).astype(kind)


def setup_inputs(seed: int = 0) -> dict:
    seeds = jax.random.split(jax.random.key(seed), 11)
    return {
        "hidden": bell_draw(seeds[0], (SEQ, MODEL_WIDTH), 1.0, 6.0, ((0, 16), (1, 16))),
        "query_frozen_projection": draw_query_frozen_projection(jax.random.fold_in(seeds[10], 71), 0),
        "key_projected": draw_key_projected(jax.random.fold_in(seeds[10], 71), 0),
        "value_frozen_projection": bell_draw(seeds[3], (SEQ, KEY_VALUE_HEADS * HEAD_SIZE), 1.0, 6.0, ((0, 16),)),
        "query_down_factor": bell_draw(seeds[4], (MODEL_WIDTH, ADAPTER_RANK), MODEL_WIDTH ** -0.5, 0.0625, ((0, 16),)),
        "query_up_factor": bell_draw(seeds[5], (ADAPTER_RANK, QUERY_HEADS * HEAD_SIZE), ADAPTER_RANK ** -0.5, 1.5, ((1, 16),)),
        "value_down_factor": bell_draw(seeds[6], (MODEL_WIDTH, ADAPTER_RANK), MODEL_WIDTH ** -0.5, 0.0625, ((0, 16),)),
        "value_up_factor": bell_draw(seeds[7], (ADAPTER_RANK, KEY_VALUE_HEADS * HEAD_SIZE), ADAPTER_RANK ** -0.5, 1.5),
        "output_gradient": bell_draw(seeds[8], (SEQ, QUERY_HEADS * HEAD_SIZE), 0.003, 0.046875, ((0, 16), (1, 16))),
        "head_shift_mask": draw_head_shift_mask(jax.random.fold_in(seeds[10], 71), 0),
    }


adapter_scale = 2.0
pos_interp = 32.0
rope_base = 10000.0


def rope_tables(positions, head_width):
    half_width = head_width // 2
    inv_freq = rope_base ** (-(jnp.arange(half_width, dtype=jnp.float32) * 2.0 / head_width))
    angles = (positions.astype(jnp.float32) / pos_interp)[:, None] * inv_freq[None, :]
    return jnp.cos(angles), jnp.sin(angles)


def rotate(tensor, cosine, sine_table):
    half_width = tensor.shape[-1] // 2
    first_half = tensor[..., :half_width]
    second_half = tensor[..., half_width:]
    return jnp.concatenate([first_half * cosine - second_half * sine_table, second_half * cosine + first_half * sine_table], axis=-1)


def unrotate(tensor, cosine, sine_table):
    half_width = tensor.shape[-1] // 2
    first_half = tensor[..., :half_width]
    second_half = tensor[..., half_width:]
    return jnp.concatenate([first_half * cosine + second_half * sine_table, second_half * cosine - first_half * sine_table], axis=-1)


def group_grads(query_rows, key_rows, value_rows, upstream):
    scale_factor = query_rows.shape[-1] ** -0.5
    scores = jnp.dot(query_rows, key_rows.T, preferred_element_type=jnp.float32) * scale_factor
    row_ids = lax.broadcasted_iota(jnp.int32, scores.shape, 0)
    col_ids = lax.broadcasted_iota(jnp.int32, scores.shape, 1)
    scores = jnp.where(col_ids <= row_ids, scores, -1e30)
    row_peak = jnp.max(scores, axis=1, keepdims=True)
    weights = jnp.exp(scores - row_peak)
    probs = weights / jnp.sum(weights, axis=1, keepdims=True)
    probs_low = probs.astype(jnp.bfloat16)
    output = jnp.dot(probs_low, value_rows, preferred_element_type=jnp.float32)
    delta = jnp.sum(upstream.astype(jnp.float32) * output, axis=1, keepdims=True)
    prob_grad = jnp.dot(upstream, value_rows.T, preferred_element_type=jnp.float32)
    score_grad = (probs * (prob_grad - delta)).astype(jnp.bfloat16)
    query_grad = jnp.dot(score_grad, key_rows, preferred_element_type=jnp.float32) * scale_factor
    value_gradient_total = jnp.dot(probs_low.T, upstream, preferred_element_type=jnp.float32)
    return query_grad, value_gradient_total


def reference(hidden, query_frozen_projection, key_projected, value_frozen_projection, query_down_factor, query_up_factor, value_down_factor, value_up_factor, output_gradient, head_shift_mask):
    highest_precision = lax.Precision.HIGHEST
    query_upstream = jnp.dot(hidden, query_down_factor, preferred_element_type=jnp.float32).astype(jnp.bfloat16)
    value_upstream = jnp.dot(hidden, value_down_factor, preferred_element_type=jnp.float32).astype(jnp.bfloat16)
    cosine, sine_table = rope_tables(jnp.arange(SEQ, dtype=jnp.int32), HEAD_SIZE)
    cos_rows = cosine[:, None, :]
    sin_rows = sine_table[:, None, :]
    query_before_rotary = query_frozen_projection.astype(jnp.float32) + adapter_scale * jnp.dot(query_upstream.astype(jnp.float32), query_up_factor.astype(jnp.float32), precision=highest_precision)
    query_all = rotate(query_before_rotary.reshape(SEQ, QUERY_HEADS, HEAD_SIZE), cos_rows, sin_rows).astype(jnp.bfloat16)
    key_all = rotate(key_projected.astype(jnp.float32).reshape(SEQ, KEY_VALUE_HEADS, HEAD_SIZE), cos_rows, sin_rows).astype(jnp.bfloat16)
    value_before_adapter = value_frozen_projection.astype(jnp.float32) + adapter_scale * jnp.dot(value_upstream.astype(jnp.float32), value_up_factor.astype(jnp.float32), precision=highest_precision)
    value_all = value_before_adapter.astype(jnp.bfloat16).reshape(SEQ, KEY_VALUE_HEADS, HEAD_SIZE)
    upstream_all = output_gradient.reshape(SEQ, QUERY_HEADS, HEAD_SIZE)
    per_kv = QUERY_HEADS // KEY_VALUE_HEADS

    def one_head(head_number):
        shifted = head_shift_mask[head_number] > 0
        kv_number = head_number // per_kv
        query_head = lax.dynamic_index_in_dim(query_all, head_number, 1, keepdims=False)
        key_head = lax.dynamic_index_in_dim(key_all, kv_number, 1, keepdims=False)
        value_head = lax.dynamic_index_in_dim(value_all, kv_number, 1, keepdims=False)
        upstream_head = lax.dynamic_index_in_dim(upstream_all, head_number, 1, keepdims=False)

        def arrange(tensor):
            rolled = jnp.where(shifted, jnp.roll(tensor, -(GROUP // 2), axis=0), tensor)
            return rolled.reshape(SEQ // GROUP, GROUP, HEAD_SIZE)

        def restore(tensor):
            flat_rows = tensor.reshape(SEQ, HEAD_SIZE)
            return jnp.where(shifted, jnp.roll(flat_rows, GROUP // 2, axis=0), flat_rows)

        query_grad, value_gradient_total = jax.vmap(group_grads)(arrange(query_head), arrange(key_head), arrange(value_head), arrange(upstream_head))
        return restore(query_grad), restore(value_gradient_total)

    query_grads, value_grads = lax.map(one_head, jnp.arange(QUERY_HEADS, dtype=jnp.int32))
    query_tok = jnp.moveaxis(query_grads, 0, 1)
    prior_gradient = unrotate(query_tok, cos_rows, sin_rows).reshape(SEQ, QUERY_HEADS * HEAD_SIZE)
    value_kv = value_grads.reshape(KEY_VALUE_HEADS, per_kv, SEQ, HEAD_SIZE).sum(axis=1)
    value_gradient_total = jnp.moveaxis(value_kv, 0, 1).reshape(SEQ, KEY_VALUE_HEADS * HEAD_SIZE)
    query_up_gradient = adapter_scale * jnp.dot(query_upstream.astype(jnp.float32).T, prior_gradient, precision=highest_precision)
    value_up_gradient = adapter_scale * jnp.dot(value_upstream.astype(jnp.float32).T, value_gradient_total, precision=highest_precision)
    token_query_gradient = (adapter_scale * jnp.dot(prior_gradient, query_up_factor.astype(jnp.float32).T, precision=highest_precision)).astype(jnp.bfloat16)
    token_value_gradient = (adapter_scale * jnp.dot(value_gradient_total, value_up_factor.astype(jnp.float32).T, precision=highest_precision)).astype(jnp.bfloat16)
    grad_a_q = jnp.dot(hidden.T, token_query_gradient, preferred_element_type=jnp.float32)
    grad_a_v = jnp.dot(hidden.T, token_value_gradient, preferred_element_type=jnp.float32)
    return (grad_a_q, query_up_gradient, grad_a_v, value_up_gradient)
```

```python
import functools

import jax
import jax.numpy as jnp
import numpy as np
from jax import lax
from jax.experimental import pallas as pl
from jax.experimental.pallas import tpu as pltpu
from jax.sharding import PartitionSpec as P

QUERY_HEADS = 64
KEY_VALUE_HEADS = 8
HEAD_SIZE = 128

adapter_scale = 2.0
pos_interp = 32.0
rope_base = 10000.0
LOG2E = 1.4426950408889634
MESH = pl.DeviceIdType.MESH
BLK = 256
HALF_HEAD = HEAD_SIZE // 2
BF = jnp.bfloat16
F32 = jnp.float32


def angle_tables(rows, groups):
    inv_freq = rope_base ** (-(np.arange(HALF_HEAD, dtype=np.float64) * 2.0 / HEAD_SIZE))
    fine = inv_freq[:, None] * (np.arange(rows, dtype=np.float64) / pos_interp)[None, :]
    coarse = inv_freq[:, None] * (np.arange(128, dtype=np.float64) * rows / pos_interp)[None, :]
    make = lambda f, x: np.asarray(f(x), dtype=np.float32)
    return make(np.cos, fine), make(np.sin, fine), make(np.cos, coarse), make(np.sin, coarse)


def nn(a, b):
    return lax.dot_general(a, b, (((1,), (0,)), ((), ())), preferred_element_type=F32)


def nt(a, b):
    return lax.dot_general(a, b, (((1,), (1,)), ((), ())), preferred_element_type=F32)


def tn(a, b):
    return lax.dot_general(a, b, (((0,), (0,)), ((), ())), preferred_element_type=F32)


def turned(x, c, s):
    top, low = x[:HALF_HEAD], x[HALF_HEAD:]
    return jnp.concatenate([top * c - low * s, low * c + top * s], axis=0)


def turned_back(x, c, s):
    top, low = x[:HALF_HEAD], x[HALF_HEAD:]
    return jnp.concatenate([top * c + low * s, low * c - top * s], axis=0)


def kernel(
    nc, nh, heads,
    hid, qf, kp, vf, qd, qu, vd, vu, dog, msk, fine_c, fine_s, coarse_c, coarse_s,
    o_aq, o_qu, o_av, o_vu,
    hidv, qfv, dov, kvown, kvprev, dnv, quv, vul, fc, fs, cc, cs,
    ub, ur, us, ug, uvp,
    qt, dt, dn, kk, kt, vv, tc, ts, tcp, tsp, uq, uv,
    tq, qacc, dv,
    tsend, trecv, tprev, tsum, tg,
    es, er, esum, eg, vg,
    gs, gr, gsum, gg,
    lsem, kvs, kvr, fws, fwr, ups, upr,
    urs_s, urs_r, uag_s, uag_r, trs_s, trs_r, tps_s, tps_r, tag_s, tag_r,
    ers_s, ers_r, eag_s, eag_r, vag_s, vag_r, grs_s, grs_r, gag_s, gag_r,
):
    c, h = lax.axis_index("ctx"), lax.axis_index("head")
    nxt, prv = lax.rem(c + 1, nc), lax.rem(c + nc - 1, nc)
    core = lax.rem(h, 2)
    sib = h + 1 - 2 * core
    kvh = h * heads // (QUERY_HEADS // KEY_VALUE_HEADS)
    kvcol = pl.ds(pl.multiple_of(kvh * HEAD_SIZE, HEAD_SIZE), HEAD_SIZE)
    m = 16 // nc

    local = [
        (hid, hidv), (kp.at[:, kvcol], kvown.at[0]), (vf.at[:, kvcol], kvown.at[1]),
        (qd, dnv.at[0]), (vd, dnv.at[1]), (fine_c, fc), (fine_s, fs), (coarse_c, cc), (coarse_s, cs),
        (qf, qfv), (dog, dov), (qu, quv), (vu.at[:, kvcol], vul),
    ]
    copies = [pltpu.make_async_copy(a, b, lsem.at[i]) for i, (a, b) in enumerate(local)]
    for i in (0, 3, 4, 1, 2, 5, 6, 7, 8, 10, 9, 11, 12):
        copies[i].start()

    bar = pltpu.get_barrier_semaphore()

    def greet(dev):
        pl.semaphore_signal(bar, inc=1, device_id=dev, device_id_type=MESH)

    @pl.loop(1, nh)
    def _(i):
        p = lax.rem(h + i, nh)
        greet((c, p))
        greet((nxt, p))
        greet((prv, p))

    @pl.loop(1, nc)
    def _(i):
        greet((lax.rem(c + i, nc), h))

    def rdma(src, dst, ssem, rsem, dev):
        return pltpu.make_async_remote_copy(
            src_ref=src, dst_ref=dst, send_sem=ssem, recv_sem=rsem, device_id=dev, device_id_type=MESH
        )

    def each(n, me, f):
        @pl.loop(1, n)
        def _(i):
            f(lax.rem(me + i, n))

    def head_rs(src, dst, ssem, rsem, p):
        return rdma(src.at[p], dst.at[h], ssem.at[p], rsem.at[h], (c, p))

    def head_from(dst, ssem, rsem, p):
        return rdma(dst.at[p], dst.at[p], ssem.at[p], rsem.at[p], (c, p))

    def head_ag(src, dst, ssem, rsem, p):
        return rdma(src, dst.at[h], ssem.at[p], rsem.at[h], (c, p))

    def ctx_from(dst, ssem, rsem, p):
        return rdma(dst.at[p], dst.at[p], ssem.at[p], rsem.at[p], (p, h))

    for i in (0, 3, 4):
        copies[i].wait()
    ut = nt(dnv[...].reshape(32, dnv.shape[2]), hidv[...])
    for p in range(16):
        r, l = p // 8, p % 8
        ub[p] = ut[16 * r:16 * r + 16, 128 * l:128 * l + 128]
    pl.semaphore_wait(bar, 3 * (nh - 1) + nc - 1)
    each(nh, h, lambda p: head_rs(ub, ur, urs_s, urs_r, p).start())

    copies[1].wait()
    copies[2].wait()
    half = kvown.shape[1] // 2
    kv_send = rdma(kvown.at[core, pl.ds(half, half)], kvprev.at[core], kvs, kvr, (nxt, h))
    kv_send.start()

    for i in (5, 6, 7, 8):
        copies[i].wait()
    lane = lax.broadcasted_iota(jnp.int32, cc.shape, 1)

    def column(tab, at):
        return jnp.sum(jnp.where(lane == at, tab, 0.0), axis=1, keepdims=True)

    def tables(at, blocks, c_ref, s_ref):
        base_c, base_s = column(cc[...], at), column(cs[...], at)
        for j, b in enumerate(blocks):
            f_c, f_s = fc[:, BLK * b:BLK * b + BLK], fs[:, BLK * b:BLK * b + BLK]
            c_ref[j] = base_c * f_c - base_s * f_s
            s_ref[j] = base_s * f_c + base_c * f_s

    tables(c, (0, 1, 2, 3), tc, ts)
    tables(prv, (2, 3), tcp, tsp)

    def key_block(raw, b, cos, sin):
        k_t = turned(raw.astype(F32).T, cos, sin).astype(BF)
        kt[b] = k_t
        kk[b] = k_t.astype(F32).T.astype(BF)

    for b in range(4):
        key_block(kvown[0, BLK * b:BLK * b + BLK], b, tc[b], ts[b])

    ur[h] = ub[h]
    each(nh, h, lambda p: head_from(ur, urs_s, urs_r, p).wait_recv())
    u_sum = ur[0]
    for p in range(1, 16):
        u_sum = u_sum + ur[p]
    us[...] = u_sum.astype(BF)
    ug[h] = us[...]
    each(nh, h, lambda p: head_ag(us, ug, uag_s, uag_r, p).start())

    copies[10].wait()
    for hd in range(heads):
        for b in range(4):
            x = dov[BLK * b:BLK * b + BLK, HEAD_SIZE * hd:HEAD_SIZE * (hd + 1)]
            dn[hd, b] = x
            dt[hd, b] = x.astype(F32).T.astype(BF)
    copies[9].wait()
    for hd in range(heads):
        for b in range(4):
            x = qfv[BLK * b:BLK * b + BLK, HEAD_SIZE * hd:HEAD_SIZE * (hd + 1)]
            qt[hd, b] = x.astype(F32).T.astype(BF)
    tq[...] = jnp.zeros_like(tq)
    dv[...] = jnp.zeros_like(dv)
    copies[11].wait()
    copies[12].wait()

    each(nh, h, lambda p: head_from(ug, uag_s, uag_r, p).wait_recv())
    u_prev_send = rdma(ug.at[pl.ds(12, 4)], uvp, ups, upr, (nxt, h))
    u_prev_send.start()
    for b in range(4):
        uq[b] = jnp.concatenate([ug[2 * b], ug[2 * b + 1]], axis=1)
        uv[b] = jnp.concatenate([ug[8 + 2 * b], ug[9 + 2 * b]], axis=1)

    kv_send.wait_recv()
    fwd = rdma(kvprev.at[core], kvprev.at[core], fws, fwr, (c, sib))
    fwd.start()

    for hd in range(heads):
        up_h = quv[:, HEAD_SIZE * hd:HEAD_SIZE * (hd + 1)]
        for b in range(4):
            q_t = qt[hd, b].astype(F32) + adapter_scale * tn(up_h, uq[b])
            qt[hd, b] = turned(q_t, tc[b], ts[b]).astype(BF)

    def value_block(raw, b):
        vv[b] = (raw.astype(F32) + adapter_scale * tn(uv[b], vul[...])).astype(BF)

    for b in range(4):
        value_block(kvown[1, BLK * b:BLK * b + BLK], b)

    scale = HEAD_SIZE ** -0.5
    sharp = scale * LOG2E
    key_at = lax.broadcasted_iota(jnp.int32, (BLK, BLK), 0)
    row_at = lax.broadcasted_iota(jnp.int32, (BLK, BLK), 1)

    def chunk(hd, qi, blocks):
        q_t, d_t = qt[hd, qi], dt[hd, qi]
        d_n = dn[hd, qi]
        scores = [nn(kk[kb], q_t) for kb in blocks]
        scores[-1] = jnp.where(key_at <= row_at, scores[-1], -1e30)
        peak = functools.reduce(jnp.maximum, [jnp.max(s, axis=0, keepdims=True) for s in scores])
        peak = peak * sharp
        weights = [jnp.exp2(s * sharp - peak) for s in scores]
        total = functools.reduce(jnp.add, [jnp.sum(w, axis=0, keepdims=True) for w in weights])
        inverse = 1.0 / total
        probs = [w * inverse for w in weights]
        prob_grad = [nn(vv[kb], d_t) for kb in blocks]
        delta = functools.reduce(
            jnp.add, [jnp.sum(p * g, axis=0, keepdims=True) for p, g in zip(probs, prob_grad)]
        )
        dvs = [nn(p.astype(BF), d_n) for p in probs]
        score_grad = [(p * (g - delta)).astype(BF) for p, g in zip(probs, prob_grad)]
        dq = functools.reduce(jnp.add, [nn(kt[kb], s) for kb, s in zip(blocks, score_grad)])
        pg = turned_back(dq, tc[qi], ts[qi]).astype(BF)
        up_h = quv[:, pl.ds(pl.multiple_of(hd * HEAD_SIZE, HEAD_SIZE), HEAD_SIZE)]
        return nn(up_h, pg), nt(uq[qi], pg), dvs

    @pl.loop(0, heads)
    def _(hd):
        shifted = msk[hd]
        on = shifted.astype(F32)
        off = 1.0 - on
        q0 = 2 * shifted
        t0, a0, d0 = chunk(hd, q0, [q0])
        t1, a1, d1 = chunk(hd, q0 + 1, [q0, q0 + 1])
        qacc[hd] = a0 + a1
        tq[0] += t0 * off
        tq[1] += t1 * off
        tq[2] += t0 * on
        tq[3] += t1 * on
        x0, x1 = d0[0] + d1[0], d1[1]
        dv[0] += x0 * off
        dv[1] += x1 * off
        dv[2] += x0 * on
        dv[3] += x1 * on

    rdma(kvprev.at[1 - core], kvprev.at[1 - core], fws, fwr, (c, sib)).wait_recv()
    for j in range(2):
        key_block(kvprev[0, BLK * j:BLK * j + BLK], 4 + j, tcp[j], tsp[j])
    u_prev_send.wait_recv()
    for j in range(2):
        uv[4 + j] = jnp.concatenate([uvp[2 * j], uvp[2 * j + 1]], axis=1)
        value_block(kvprev[1, BLK * j:BLK * j + BLK], 4 + j)

    @pl.loop(0, heads)
    def _(hd):
        shifted = msk[hd]
        on = shifted.astype(F32)
        off = 1.0 - on
        q0 = 2 - 2 * shifted
        far = 4 * shifted
        t0, a0, d0 = chunk(hd, q0, [far, far + 1, q0])
        t1, a1, d1 = chunk(hd, q0 + 1, [far, far + 1, q0, q0 + 1])
        qacc[hd] += a0 + a1
        tq[0] += t0 * on
        tq[1] += t1 * on
        tq[2] += t0 * off
        tq[3] += t1 * off
        f0, f1 = d0[0] + d1[0], d0[1] + d1[1]
        x0, x1 = d0[2] + d1[2], d1[3]
        dv[0] += x0 * on + f0 * off
        dv[1] += x1 * on + f1 * off
        dv[2] += x0 * off
        dv[3] += x1 * off
        dv[4] += f0 * on
        dv[5] += f1 * on

    v_acc = jnp.zeros((16, HEAD_SIZE), F32)
    for b in range(6):
        dv_b = dv[b].astype(BF)
        t_v = (adapter_scale * nt(vul[...], dv_b)).astype(BF)
        v_acc = v_acc + nn(uv[b], dv_b)
        tsend[8 + 2 * b] = t_v[:, :128]
        tsend[9 + 2 * b] = t_v[:, 128:]
    for b in range(4):
        t_q = (adapter_scale * scale * tq[b]).astype(BF)
        tsend[2 * b] = t_q[:, :128]
        tsend[2 * b + 1] = t_q[:, 128:]

    def prev_send(k):
        return rdma(tsend.at[16 + k], tprev.at[h], tps_s.at[k], tps_r.at[h], (prv, 12 + k))

    for k in range(4):
        prev_send(k).start()
    each(nh, h, lambda p: head_rs(tsend, trecv, trs_s, trs_r, p).start())

    for l in range(heads):
        a = adapter_scale * scale * qacc[l]
        es[l] = a[:8]
        es[4 + l] = a[8:]
    es[8] = adapter_scale * v_acc[:8]
    es[9] = adapter_scale * v_acc[8:]

    def ctx_rs(src, dst, ssem, rsem, p):
        return rdma(src.at[pl.ds(p * m, m)], dst.at[c], ssem.at[p], rsem.at[c], (p, h))

    def ctx_ag(src, dst, ssem, rsem, p):
        return rdma(src, dst.at[pl.ds(c * m, m)], ssem.at[p], rsem.at[c], (p, h))

    def ctx_piece_from(dst, ssem, rsem, p):
        return rdma(dst.at[pl.ds(p * m, m)], dst.at[pl.ds(p * m, m)], ssem.at[p], rsem.at[p], (p, h))

    def if_early(p, f):
        @pl.when(p * m < 10)
        def _():
            f(p)

    each(nc, c, lambda p: if_early(p, lambda p: ctx_rs(es, er, ers_s, ers_r, p).start()))

    trecv[h] = tsend[h]
    each(nh, h, lambda p: head_from(trecv, trs_s, trs_r, p).wait_recv())
    t_sum = trecv[0].astype(F32)
    for p in range(1, 16):
        t_sum = t_sum + trecv[p].astype(F32)

    @pl.when(h < 12)
    def _():
        tsum[...] = t_sum.astype(BF)

    @pl.when(h >= 12)
    def _():
        @pl.loop(0, nh)
        def _(p):
            rdma(tprev.at[p], tprev.at[p], tps_s.at[0], tps_r.at[p], (nxt, p)).wait_recv()

        extra = t_sum
        for p in range(16):
            extra = extra + tprev[p].astype(F32)
        tsum[...] = extra.astype(BF)

    tg[h] = tsum[...]
    each(nh, h, lambda p: head_ag(tsum, tg, tag_s, tag_r, p).start())

    def early_sum(p):
        er[p] = es[pl.ds(p * m, m)]
        each(nc, c, lambda p: ctx_from(er, ers_s, ers_r, p).wait_recv())
        e_sum = er[0]
        for j in range(1, nc):
            e_sum = e_sum + er[j]
        esum[...] = e_sum
        eg[pl.ds(p * m, m)] = e_sum
        each(nc, c, lambda p: ctx_ag(esum, eg, eag_s, eag_r, p).start())

    if_early(c, early_sum)

    each(nh, h, lambda p: head_from(tg, tag_s, tag_r, p).wait_recv())
    t_all = jnp.concatenate(
        [
            jnp.concatenate([tg[8 * r + l] for l in range(8)], axis=1)
            for r in range(2)
        ],
        axis=0,
    )
    grad = nn(t_all, hidv[...])
    for p in range(16):
        r, l = p // 4, p % 4
        gs[p] = grad[8 * r:8 * r + 8, 128 * l:128 * l + 128]
    each(nc, c, lambda p: ctx_rs(gs, gr, grs_s, grs_r, p).start())

    each(nc, c, lambda p: if_early(p, lambda p: ctx_piece_from(eg, eag_s, eag_r, p).wait_recv()))
    v_part = eg.at[pl.ds(8, 2)]
    each(nh, h, lambda p: head_ag(v_part, vg, vag_s, vag_r, p).start())
    for l in range(heads):
        o_qu[:8, 128 * l:128 * l + 128] = eg[l]
        o_qu[8:, 128 * l:128 * l + 128] = eg[4 + l]
    vg[h] = eg[8:10]

    gr[c] = gs[pl.ds(c * m, m)]
    each(nc, c, lambda p: ctx_from(gr, grs_s, grs_r, p).wait_recv())
    g_sum = gr[0]
    for j in range(1, nc):
        g_sum = g_sum + gr[j]
    gsum[...] = g_sum
    gg[pl.ds(c * m, m)] = g_sum
    each(nc, c, lambda p: ctx_ag(gsum, gg, gag_s, gag_r, p).start())

    each(nh, h, lambda p: head_from(vg, vag_s, vag_r, p).wait_recv())
    per = nh // KEY_VALUE_HEADS
    for k in range(KEY_VALUE_HEADS):
        s = vg[k * per]
        for j in range(1, per):
            s = s + vg[k * per + j]
        o_vu[:8, 128 * k:128 * k + 128] = s[0]
        o_vu[8:, 128 * k:128 * k + 128] = s[1]

    kv_send.wait_send()
    fwd.wait_send()
    u_prev_send.wait_send()
    for k in range(4):
        prev_send(k).wait_send()

    def head_sent(p):
        head_rs(ub, ur, urs_s, urs_r, p).wait_send()
        head_ag(us, ug, uag_s, uag_r, p).wait_send()
        head_rs(tsend, trecv, trs_s, trs_r, p).wait_send()
        head_ag(tsum, tg, tag_s, tag_r, p).wait_send()
        head_ag(v_part, vg, vag_s, vag_r, p).wait_send()

    each(nh, h, head_sent)

    def ctx_sent(p):
        if_early(p, lambda p: ctx_rs(es, er, ers_s, ers_r, p).wait_send())
        ctx_rs(gs, gr, grs_s, grs_r, p).wait_send()
        ctx_ag(gsum, gg, gag_s, gag_r, p).wait_send()

    each(nc, c, ctx_sent)
    if_early(c, lambda _: each(nc, c, lambda p: ctx_ag(esum, eg, eag_s, eag_r, p).wait_send()))

    each(nc, c, lambda p: ctx_piece_from(gg, gag_s, gag_r, p).wait_recv())
    for p in range(16):
        r, l = p // 4, p % 4
        out = o_aq if r < 2 else o_av
        out[8 * (r % 2):8 * (r % 2) + 8, 128 * l:128 * l + 128] = gg[p]


def on_device(nc, nh, hidden, qf, kp, vf, qd, qu, vd, vu, dog, mask):
    rows, width = hidden.shape
    heads = mask.shape[0]
    m = 16 // nc
    half = rows // 2
    fine_c, fine_s, coarse_c, coarse_s = angle_tables(rows, nc)
    vm = pltpu.VMEM
    dma = pltpu.SemaphoreType.DMA
    hsem, csem = dma((nh,)), dma((nc,))
    any_spec = pl.BlockSpec(memory_space=pl.ANY)
    vmem_spec = pl.BlockSpec(memory_space=pltpu.VMEM)
    out = pl.pallas_call(
        functools.partial(kernel, nc, nh, heads),
        out_shape=(
            jax.ShapeDtypeStruct((16, width), F32),
            jax.ShapeDtypeStruct((16, width), F32),
            jax.ShapeDtypeStruct((16, width), F32),
            jax.ShapeDtypeStruct((16, KEY_VALUE_HEADS * HEAD_SIZE), F32),
        ),
        in_specs=[any_spec] * 9 + [pl.BlockSpec(memory_space=pltpu.SMEM)] + [any_spec] * 4,
        out_specs=(vmem_spec,) * 4,
        scratch_shapes=[
            vm((rows, width), BF), vm((rows, width), BF), vm((rows, width), BF),
            vm((2, rows, HEAD_SIZE), BF), vm((2, half, HEAD_SIZE), BF),
            vm((2, 16, width), BF), vm((16, width), BF), vm((16, HEAD_SIZE), BF),
            vm((HALF_HEAD, rows), F32), vm((HALF_HEAD, rows), F32),
            vm((HALF_HEAD, 128), F32), vm((HALF_HEAD, 128), F32),
            vm((16, 16, 128), F32), vm((16, 16, 128), F32), vm((16, 128), BF),
            vm((16, 16, 128), BF), vm((4, 16, 128), BF),
            vm((heads, 4, HEAD_SIZE, BLK), BF), vm((heads, 4, HEAD_SIZE, BLK), BF),
            vm((heads, 4, BLK, HEAD_SIZE), BF),
            vm((6, BLK, HEAD_SIZE), BF), vm((6, HEAD_SIZE, BLK), BF), vm((6, BLK, HEAD_SIZE), BF),
            vm((4, HALF_HEAD, BLK), F32), vm((4, HALF_HEAD, BLK), F32),
            vm((2, HALF_HEAD, BLK), F32), vm((2, HALF_HEAD, BLK), F32),
            vm((4, 16, BLK), BF), vm((6, 16, BLK), BF),
            vm((4, 16, BLK), F32), vm((heads, 16, HEAD_SIZE), F32), vm((6, BLK, HEAD_SIZE), F32),
            vm((20, 16, 128), BF), vm((16, 16, 128), BF), vm((16, 16, 128), BF),
            vm((16, 128), BF), vm((16, 16, 128), BF),
            vm((16, 8, 128), F32), vm((nc, m, 8, 128), F32), vm((m, 8, 128), F32),
            vm((16, 8, 128), F32), vm((16, 2, 8, 128), F32),
            vm((16, 8, 128), F32), vm((nc, m, 8, 128), F32), vm((m, 8, 128), F32), vm((16, 8, 128), F32),
            dma((13,)), dma, dma, dma, dma, dma, dma,
            hsem, hsem, hsem, hsem, hsem, hsem, dma((4,)), hsem, hsem, hsem,
            csem, csem, csem, csem, hsem, hsem, csem, csem, csem, csem,
        ],
        compiler_params=pltpu.CompilerParams(
            collective_id=0, has_side_effects=True, vmem_limit_bytes=56 * 1024 * 1024
        ),
        name="adapter_grads",
    )(hidden, qf, kp, vf, qd.T, qu, vd.T, vu, dog, mask, fine_c, fine_s, coarse_c, coarse_s)
    a_q, q_up, a_v, v_up = out
    return a_q.T, q_up, a_v.T, v_up


def solution(mesh):
    nc, nh = mesh.shape["ctx"], mesh.shape["head"]
    return jax.shard_map(
        functools.partial(on_device, nc, nh),
        mesh=mesh,
        in_specs=(
            P("ctx", "head"),
            P("ctx", "head"),
            P("ctx", None),
            P("ctx", None),
            P("head", None),
            P(None, "head"),
            P("head", None),
            P(),
            P("ctx", "head"),
            P("head"),
        ),
        out_specs=(P("head", None), P(None, "head"), P("head", None), P()),
        check_vma=False,
    )
```
